32 devices in a mesh: groups: 2 (over x), expert: 16 (over z, y, core).
Axes of the slice: x: 2, y: 2, z: 4, core: 2. Of those that a mesh axis runs over, the one named last changes fastest.
Arguments:
- tokens: bfloat16 [4096, 2048], P(('groups', 'expert')), parts along dimension 0, may hold values from -6 to 6
- stream_type: int32 [4096], P(('groups', 'expert')), parts along dimension 0, may hold values from 0 to 1
- norm_gain: float32 [2, 2048], replicated, may hold values from 0.1 to 1.9
- expert_ids: int32 [4096, 8], P(('groups', 'expert')), parts along dimension 0, may hold values from 0 to 31, all different within a row; in each aligned block of 128 rows (0 to 127, 128 to 255, ...) at most 40 rows name the same one
- gate_weights: float32 [4096, 8], P(('groups', 'expert')), parts along dimension 0, may hold values from 0.03 to 0.4
- w_gate: bfloat16 [32, 2048, 384], P('expert'), may hold values from -0.125 to 0.125
- w_up: bfloat16 [32, 2048, 384], P('expert'), may hold values from -0.125 to 0.125
- w_down: bfloat16 [32, 384, 2048], P('expert'), may hold values from -0.3125 to 0.3125
- cotangent: bfloat16 [4096, 2048], P(('groups', 'expert')), parts along dimension 0, may hold values from -6 to 6
Outputs:
- moe_out: bfloat16 [4096, 2048], P(('groups', 'expert')), parts along dimension 0
- grad_input: bfloat16 [4096, 2048], P(('groups', 'expert')), parts along dimension 0
The draws below stay inside these ranges and needn't reach their ends.
There are 2 independent parts, one for each index of `groups`. The reference program is written for one: setup_inputs(seed, part) draws one part's arguments, and reference() takes and returns one part's arrays. A program takes and returns all parts, laid end to end along the dimension named above; an argument that names none is the same for every part. Nothing has to cross between parts.
Inputs may be any that keep to these rules, and one draw needn't show every extreme that they name: `expert_ids`: among the 128 tokens of one device no expert is named more than 40 times, a bound that some block reaches; the 8 experts of a token are different.
All inputs are finite; a program needn't handle non-finite values.
Results may differ from the reference program's by a relative error of at most 0.0071.
Values may be sent and summed in bfloat16 or wider, within the bound.
A program may use at most 128 MiB of HBM per device.

```python
import math
import jax
import jax.numpy as jnp
import numpy as np
from jax import lax

D = 2048
FF = 384
TOPK = 8
TOK_DEV = 128
EXPERTS = 32
CAP = 40
TOKENS = 2048
N_EXPERT = 16


def touch_ends(result, rng, smallest, top_value):
    extent = result.shape
    place = [jax.random.randint(jax.random.fold_in(rng, axis), (), 0, extent[axis]) for axis in range(len(extent))]
    result = result.at[tuple(place)].set(smallest)
    longest = extent.index(max(extent))
    place[longest] = (place[longest] + 1) % extent[longest]
    return result.at[tuple(place)].set(top_value)


def level_of(key, shape, shards, smallest, largest):
    def one(position, parts):
        draws = jax.random.uniform(jax.random.fold_in(jax.random.fold_in(key, 6), position), (parts,), jnp.float32, smallest / len(shards), largest / len(shards))
        return jnp.repeat(jnp.exp(draws), shape[position] // parts).reshape((-1,) + (1,) * (len(shape) - position - 1))

    gain = one(*shards[0])
    for cut in shards[1:]:
        gain = gain * one(*cut)
    return gain


def shared_out(rng, own, number, rows, count, top, most, skew):
    ranking = jax.random.permutation(rng, count)
    heavy_load, ordinary = load_shares(count, rows * top, most, skew, True), load_shares(count, rows * top, most, skew, False)
    places = jnp.arange(count)

    def named(lengths, turn):
        used = int((lengths > 0).sum())
        fixed = max(1, used // 4)
        moved = fixed + (places - fixed + turn * (used - fixed)) % max(1, count - fixed)
        return jnp.zeros((count,), jnp.int32).at[ranking[jnp.where(places < fixed, places, moved)]].set(jnp.asarray(lengths, jnp.int32))

    lengths = jnp.where(number % 4 == 0, named(heavy_load, number // 4), named(ordinary, number - number // 4 - 1))
    mixed = jax.random.permutation(jax.random.fold_in(own, 3), count)
    donor, sink = mixed[0:count // 2 * 2:2], mixed[1:count // 2 * 2:2]
    margin = jnp.minimum(lengths[donor] - 1, most - lengths[sink]) // 2
    margin = jnp.where((donor == ranking[0]) | (sink == ranking[0]) | (lengths[sink] == 0), 0, jnp.maximum(margin, 0))
    moved = jax.random.randint(jax.random.fold_in(own, 4), (count // 2,), 0, 1 << 20) % (margin + 1)
    lengths = lengths.at[donor].add(-moved).at[sink].add(moved)
    items = jnp.searchsorted(jnp.cumsum(lengths), jnp.arange(rows * top), side="right").astype(jnp.int32)
    grid = items.reshape(top, rows).T
    grid = grid[jax.random.permutation(jax.random.fold_in(own, 1), rows)]
    turn = jax.random.randint(jax.random.fold_in(own, 2), (rows, 1), 0, top)
    return jnp.take_along_axis(grid, (jnp.arange(top)[None, :] + turn) % top, axis=1)


def load_shares(count, total, bound, lean, full):
    loads = [(1 << 20) // math.isqrt(standing ** lean) + 1 for standing in range(1, count + 1)]
    largest = bound if full else min(bound, max(-(-total // count), total * loads[0] // sum(loads)))
    least = 1 if total - largest >= count - 1 else 0
    counts, spare = [largest] + [least] * (count - 1), total - largest - least * (count - 1)
    while spare > 0:
        movable = [i for i in range(1, count) if counts[i] < largest] or [i for i in range(1, count) if counts[i] < bound]
        mass, remaining = sum([loads[i] for i in movable]), spare
        for i in movable:
            more = min(bound - counts[i], max(1, remaining * loads[i] // mass), spare)
            counts[i] = counts[i] + more
            spare = spare - more
    return np.array(counts)


def gaussian(key, extent, scale, reach, split=(), held_as=jnp.bfloat16):
    values = scale * jax.random.normal(key, extent, jnp.float32)
    if split:
        values = values * level_of(key, extent, split, -0.22, 0.18)
    return jnp.clip(values, -reach, reach).astype(held_as)


def setup_inputs(seed: int = 0, part: int = 0) -> dict:
    seeds = jax.random.split(jax.random.key(seed), 10)
    part_splits = jax.random.split(jax.random.fold_in(seeds[9], part), 10)
    tokens = gaussian(part_splits[0], (TOKENS, D), 1.0, 6.0, ((0, 16),))
    stream_type = touch_ends(jax.random.randint(part_splits[1], (TOKENS,), 0, 2), jax.random.fold_in(part_splits[1], 1), 0, 1).astype(jnp.int32)
    norm_gain = jnp.clip(1.0 + 0.18 * jax.random.normal(seeds[2], (2, D), jnp.float32), 0.1, 1.9)
    expert_ids_keys = jax.random.split(jax.random.fold_in(part_splits[3], 1), TOKENS // TOK_DEV)
    expert_ids_turns = jax.random.permutation(jax.random.fold_in(part_splits[3], 3), TOKENS // TOK_DEV)
    expert_ids = jax.vmap(lambda own, number: shared_out(jax.random.fold_in(part_splits[3], 2), own, number, TOK_DEV, EXPERTS, TOPK, CAP, 2))(expert_ids_keys, expert_ids_turns).reshape((TOKENS, TOPK))
    gate_weights = jnp.clip(jnp.exp(math.log(0.4) - 2.5902672 * jax.random.uniform(part_splits[4], (TOKENS, TOPK), jnp.float32) ** level_of(part_splits[4], (TOKENS, TOPK), ((0, 16),), -0.2, 0.2)), 0.03, 0.4)
    w_gate = gaussian(seeds[5], (EXPERTS, D, FF), D ** -0.5, 0.125, ((0, 16),))
    w_up = gaussian(seeds[6], (EXPERTS, D, FF), D ** -0.5, 0.125, ((0, 16),))
    w_down = gaussian(seeds[7], (EXPERTS, FF, D), FF ** -0.5, 0.3125, ((0, 16),))
    cotangent = gaussian(part_splits[8], (TOKENS, D), 1.0, 6.0, ((0, 16),))
    return {"tokens": tokens, "stream_type": stream_type, "norm_gain": norm_gain, "expert_ids": expert_ids, "gate_weights": gate_weights, "w_gate": w_gate, "w_up": w_up, "w_down": w_down, "cotangent": cotangent}


def reference(tokens, stream_type, norm_gain, expert_ids, gate_weights, w_gate, w_up, w_down, cotangent):
    values = tokens.astype(jnp.float32)
    inv_rms = lax.rsqrt(lax.optimization_barrier(jnp.mean(values * values, axis=-1, keepdims=True)) + 1e-06)
    unit_rows = values * inv_rms
    gain_rows = jnp.where(stream_type[:, None] == 0, norm_gain[0][None, :], norm_gain[1][None, :])
    normed = (unit_rows * gain_rows).astype(jnp.bfloat16)
    row_count = TOK_DEV * TOPK
    block_ids = expert_ids.reshape(N_EXPERT, row_count)
    onehot = (block_ids[:, :, None] == jnp.arange(EXPERTS, dtype=jnp.int32)[None, None, :]).astype(jnp.int32)
    slot_rank = lax.optimization_barrier(jnp.sum((jnp.cumsum(onehot, axis=1) - onehot) * onehot, axis=2))
    source = jnp.arange(N_EXPERT, dtype=jnp.int32)[:, None]
    slot_index = (block_ids * (N_EXPERT * CAP) + source * CAP + slot_rank).reshape(-1)
    total_rows = TOKENS * TOPK
    slot_table = jnp.full((EXPERTS * N_EXPERT * CAP,), total_rows, jnp.int32)
    slot_table = slot_table.at[slot_index].set(jnp.arange(total_rows, dtype=jnp.int32))
    slot_table = slot_table.reshape(EXPERTS, N_EXPERT * CAP)
    normed_ext = jnp.concatenate([normed, jnp.zeros((1, D), jnp.bfloat16)], axis=0)
    cot_ext = jnp.concatenate([cotangent, jnp.zeros((1, D), jnp.bfloat16)], axis=0)
    gate_flat = jnp.concatenate([gate_weights.reshape(-1), jnp.zeros((1,), jnp.float32)], axis=0)

    def per_expert(running, inputs):
        out_total, grad_total = running
        row_index, gate_mat, up_mat, down_mat = inputs
        token_index = (row_index // TOPK).astype(jnp.int32)
        row_values = normed_ext[token_index]
        gate_pre = jnp.dot(row_values, gate_mat, preferred_element_type=jnp.float32)
        up_pre = jnp.dot(row_values, up_mat, preferred_element_type=jnp.float32)
        sig_gate = jax.nn.sigmoid(gate_pre)
        active = gate_pre * sig_gate
        hidden = (active * up_pre).astype(jnp.bfloat16)
        results = jnp.dot(hidden, down_mat, preferred_element_type=jnp.float32).astype(jnp.bfloat16)
        weight_rows = gate_flat[row_index]
        out_grad = (weight_rows[:, None] * cot_ext[token_index].astype(jnp.float32)).astype(jnp.bfloat16)
        hidden_grad = jnp.dot(out_grad, down_mat.T, preferred_element_type=jnp.float32)
        pre_grad = (hidden_grad * up_pre * sig_gate * (1.0 + gate_pre * (1.0 - sig_gate))).astype(jnp.bfloat16)
        up_grad = (hidden_grad * active).astype(jnp.bfloat16)
        row_grad = (jnp.dot(pre_grad, gate_mat.T, preferred_element_type=jnp.float32) + jnp.dot(up_grad, up_mat.T, preferred_element_type=jnp.float32)).astype(jnp.bfloat16)
        out_total = out_total.at[token_index].add(weight_rows[:, None] * results.astype(jnp.float32))
        grad_total = grad_total.at[token_index].add(row_grad.astype(jnp.float32))
        return ((out_total, grad_total), None)
    start = (jnp.zeros((TOKENS + 1, D), jnp.float32), jnp.zeros((TOKENS + 1, D), jnp.float32))
    (out_total, grad_total), unused = lax.scan(per_expert, start, (slot_table, w_gate, w_up, w_down))
    moe_out = out_total[:TOKENS].astype(jnp.bfloat16)
    scaled = grad_total[:TOKENS] * gain_rows
    grad_input = inv_rms * (scaled - unit_rows * lax.optimization_barrier(jnp.mean(scaled * unit_rows, axis=-1, keepdims=True)))
    return (moe_out, grad_input.astype(jnp.bfloat16))
```

```python
import functools

import jax
import jax.numpy as jnp
from jax import lax
from jax.experimental import pallas as pl
from jax.experimental.pallas import tpu as pltpu
from jax.sharding import PartitionSpec as P

SLOTS = 1280
BF16 = jnp.bfloat16
F32 = jnp.float32


def dot(a, b, dims=((1,), (0,))):
    return lax.dot_general(a, b, (dims, ((), ())), preferred_element_type=F32)


def pick_table(ids, gates, first_expert, experts, cap, block):
    top, pair = ids.shape
    rows_i = lax.broadcasted_iota(jnp.int32, (pair, pair), 0)
    cols_i = lax.broadcasted_iota(jnp.int32, (pair, pair), 1)
    before = ((rows_i < cols_i) & ((rows_i < block) == (cols_i < block))).astype(BF16)
    masks = []
    weights = []
    for e in range(experts):
        hit = ids == (first_expert + e)
        masks.append(jnp.sum(hit.astype(F32), axis=0, keepdims=True))
        weights.append(jnp.sum(jnp.where(hit, gates, 0.0), axis=0, keepdims=True))
    lane = lax.broadcasted_iota(jnp.int32, (1, pair), 1)
    half = jnp.where(lane < block, 0, cap)
    slot_i = lax.broadcasted_iota(jnp.int32, (2 * cap, pair), 0)
    tables = []
    slot_weights = []
    for e in range(experts):
        rank = dot(jnp.broadcast_to(masks[e], (16, pair)).astype(BF16), before)[0:1].astype(jnp.int32)
        slot = jnp.where(masks[e] > 0.5, rank + half, -1)
        table = slot_i == slot
        tables.append(table.astype(F32))
        slot_weights.append(jnp.sum(jnp.where(table, weights[e], 0.0), axis=1, keepdims=True))
    return tables, slot_weights


def fwd_kernel(experts, cap, block, pairs, rows_ref, meta_ref, wg_ref, wu_ref, wd_ref,
               out_ref, gate_ref, up_ref, tab_ref, sw_ref, picked, weighted):
    first = lax.axis_index("expert") * experts
    top = meta_ref.shape[1] // 2
    n = 2 * cap
    for p in range(pairs):
        ids = meta_ref[p, 0:top, :]
        gates = meta_ref[p, top:, :]
        tables, slot_weights = pick_table(ids, gates, first.astype(F32), experts, cap, block)
        full = jnp.concatenate(tables, axis=0).astype(BF16)
        tab_ref[p] = full
        got = dot(full, rows_ref[p * 2 * block:(p + 1) * 2 * block, :]).astype(BF16)
        for e in range(experts):
            picked[e, p * n:(p + 1) * n, :] = got[e * n:(e + 1) * n]
            sw_ref[e, p * n:(p + 1) * n, :] = slot_weights[e]
    for e in range(experts):
        gate = dot(picked[e], wg_ref[e])
        up = dot(picked[e], wu_ref[e])
        gate_ref[e] = gate
        up_ref[e] = up
        hidden = (gate * jax.nn.sigmoid(gate) * up).astype(BF16)
        res = dot(hidden, wd_ref[e]) * sw_ref[e]
        res = res.astype(BF16)
        for p in range(pairs):
            weighted[p, e * n:(e + 1) * n, :] = res[p * n:(p + 1) * n]
    for p in range(pairs):
        out_ref[p * 2 * block:(p + 1) * 2 * block, :] = dot(
            tab_ref[p], weighted[p], ((0,), (0,))).astype(BF16)


def bwd_kernel(experts, cap, block, pairs, cot_ref, gate_ref, up_ref, tab_ref, sw_ref,
               wg_ref, wu_ref, wd_ref, out_ref, picked, weighted):
    n = 2 * cap
    tr = ((1,), (1,))
    for p in range(pairs):
        got = dot(tab_ref[p], cot_ref[p * 2 * block:(p + 1) * 2 * block, :])
        for e in range(experts):
            picked[e, p * n:(p + 1) * n, :] = (
                got[e * n:(e + 1) * n] * sw_ref[e, p * n:(p + 1) * n, :]).astype(BF16)
    for e in range(experts):
        hidden_grad = dot(picked[e], wd_ref[e], tr)
        gate = gate_ref[e]
        up = up_ref[e]
        sig = jax.nn.sigmoid(gate)
        pre_grad = (hidden_grad * up * sig * (1.0 + gate * (1.0 - sig))).astype(BF16)
        up_grad = (hidden_grad * gate * sig).astype(BF16)
        res = (dot(pre_grad, wg_ref[e], tr) + dot(up_grad, wu_ref[e], tr)).astype(BF16)
        for p in range(pairs):
            weighted[p, e * n:(e + 1) * n, :] = res[p * n:(p + 1) * n]
    for p in range(pairs):
        out_ref[p * 2 * block:(p + 1) * 2 * block, :] = dot(
            tab_ref[p], weighted[p], ((0,), (0,))).astype(BF16)


def expert_calls(meta, weights, block, cap, step_pairs):
    w_gate, w_up, w_down = weights
    experts, width, ff = w_gate.shape
    all_pairs, top2, pair = meta.shape
    grid = (all_pairs // step_pairs,)
    n = 2 * cap
    rows_spec = pl.BlockSpec((step_pairs * pair, width), lambda i: (i, 0))
    whole = lambda a: pl.BlockSpec(a.shape, lambda i: (0, 0, 0), pipeline_mode=pl.Buffered(1))
    pre_spec = pl.BlockSpec((experts, step_pairs * n, ff), lambda i: (0, i, 0))
    tab_spec = pl.BlockSpec((step_pairs, experts * n, pair), lambda i: (i, 0, 0))
    sw_spec = pl.BlockSpec((experts, step_pairs * n, 1), lambda i: (0, i, 0))
    pre_shape = jax.ShapeDtypeStruct((experts, all_pairs * n, ff), F32)
    scratch = [pltpu.VMEM((experts, step_pairs * n, width), BF16),
               pltpu.VMEM((step_pairs, experts * n, width), BF16)]
    params = pltpu.CompilerParams(vmem_limit_bytes=60 << 20)
    flops = 2 * 3 * experts * all_pairs * n * width * ff
    cost = pl.CostEstimate(flops=2 * flops, bytes_accessed=30 << 20, transcendentals=0)

    def fwd(rows):
        return pl.pallas_call(
            functools.partial(fwd_kernel, experts, cap, block, step_pairs),
            grid=grid,
            in_specs=[rows_spec, pl.BlockSpec((step_pairs, top2, pair), lambda i: (i, 0, 0)),
                      whole(w_gate), whole(w_up), whole(w_down)],
            out_specs=[rows_spec, pre_spec, pre_spec, tab_spec, sw_spec],
            out_shape=[jax.ShapeDtypeStruct(rows.shape, BF16), pre_shape, pre_shape,
                       jax.ShapeDtypeStruct((all_pairs, experts * n, pair), BF16),
                       jax.ShapeDtypeStruct((experts, all_pairs * n, 1), F32)],
            scratch_shapes=scratch, compiler_params=params, cost_estimate=cost,
        )(rows, meta, w_gate, w_up, w_down)

    def bwd(cots, gate_pre, up_pre, table, slot_weights):
        return pl.pallas_call(
            functools.partial(bwd_kernel, experts, cap, block, step_pairs),
            grid=grid,
            in_specs=[rows_spec, pre_spec, pre_spec, tab_spec, sw_spec,
                      whole(w_gate), whole(w_up), whole(w_down)],
            out_specs=rows_spec,
            out_shape=jax.ShapeDtypeStruct(cots.shape, BF16),
            scratch_shapes=scratch, compiler_params=params, cost_estimate=cost,
        )(cots, gate_pre, up_pre, table, slot_weights, w_gate, w_up, w_down)

    return fwd, bwd


def local(
    tokens, stream_type, norm_gain, expert_ids, gate_weights, w_gate, w_up, w_down, cotangent
):
    block, width = tokens.shape
    top = expert_ids.shape[1]
    devices = lax.axis_size("expert")
    experts_all = w_gate.shape[0] * devices
    cap = -(-(SLOTS // experts_all) // 8) * 8
    values = tokens.astype(F32)
    inv_rms = lax.rsqrt(jnp.mean(values * values, axis=-1, keepdims=True) + 1e-06)
    unit_rows = values * inv_rms
    gain_rows = jnp.where(stream_type[:, None] == 0, norm_gain[0][None, :], norm_gain[1][None, :])
    normed = (unit_rows * gain_rows).astype(BF16)
    meta = jnp.concatenate([expert_ids.astype(F32).T, gate_weights.T], axis=0)
    meta = lax.all_gather(meta, "expert", axis=0, tiled=False)
    meta = meta.reshape(devices // 2, 2, 2 * top, block).swapaxes(1, 2).reshape(
        devices // 2, 2 * top, 2 * block)
    rows = lax.all_gather(normed, "expert", axis=0, tiled=True)
    cots = lax.all_gather(cotangent, "expert", axis=0, tiled=True)
    fwd, bwd = expert_calls(meta, (w_gate, w_up, w_down), block, cap, 4)
    out_part, gate_pre, up_pre, table, slot_weights = fwd(rows)
    moe_out = lax.psum_scatter(out_part, "expert", scatter_dimension=0, tiled=True)
    grad_part = bwd(cots, gate_pre, up_pre, table, slot_weights)
    normed_grad = lax.psum_scatter(grad_part, "expert", scatter_dimension=0, tiled=True)
    scaled = normed_grad.astype(F32) * gain_rows
    grad_input = inv_rms * (
        scaled - unit_rows * jnp.mean(scaled * unit_rows, axis=-1, keepdims=True)
    )
    return (moe_out, grad_input.astype(BF16))


def solution(mesh):
    in_specs = (
        P(("groups", "expert"), None),
        P(("groups", "expert")),
        P(),
        P(("groups", "expert"), None),
        P(("groups", "expert"), None),
        P("expert", None, None),
        P("expert", None, None),
        P("expert", None, None),
        P(("groups", "expert"), None),
    )
    out_specs = (P(("groups", "expert"), None), P(("groups", "expert"), None))
    return jax.shard_map(local, mesh=mesh, in_specs=in_specs, out_specs=out_specs, check_vma=False)
```

```python
import functools

import jax
import jax.numpy as jnp
from jax import lax
from jax.experimental import pallas as pl
from jax.experimental.pallas import tpu as pltpu
from jax.sharding import PartitionSpec as P

SLOTS = 1280
BF16 = jnp.bfloat16
F32 = jnp.float32


def dot(a, b, dims=((1,), (0,))):
    return lax.dot_general(a, b, (dims, ((), ())), preferred_element_type=F32)


def pick_table(ids, gates, first_expert, experts, cap, block):
    top, pair = ids.shape
    rows_i = lax.broadcasted_iota(jnp.int32, (pair, pair), 0)
    cols_i = lax.broadcasted_iota(jnp.int32, (pair, pair), 1)
    before = ((rows_i < cols_i) & ((rows_i < block) == (cols_i < block))).astype(BF16)
    masks = []
    weights = []
    for e in range(experts):
        hit = ids == (first_expert + e)
        masks.append(jnp.sum(hit.astype(F32), axis=0, keepdims=True))
        weights.append(jnp.sum(jnp.where(hit, gates, 0.0), axis=0, keepdims=True))
    lane = lax.broadcasted_iota(jnp.int32, (1, pair), 1)
    half = jnp.where(lane < block, 0, cap)
    slot_i = lax.broadcasted_iota(jnp.int32, (2 * cap, pair), 0)
    tables = []
    slot_weights = []
    for e in range(experts):
        rank = dot(jnp.broadcast_to(masks[e], (16, pair)).astype(BF16), before)[0:1].astype(jnp.int32)
        slot = jnp.where(masks[e] > 0.5, rank + half, -1)
        table = slot_i == slot
        tables.append(table.astype(F32))
        slot_weights.append(jnp.sum(jnp.where(table, weights[e], 0.0), axis=1, keepdims=True))
    return tables, slot_weights


def fwd_kernel(experts, cap, block, pairs, top, rows_ref, wg_ref, wu_ref, wd_ref,
               out_ref, gate_ref, up_ref, tab_ref, sw_ref, picked, weighted):
    first = lax.axis_index("expert") * experts
    width = wg_ref.shape[1]
    n = 2 * cap
    for p in range(pairs):
        meta = rows_ref[p * 2 * block:(p + 1) * 2 * block, width:].astype(F32).T
        ids = meta[0:top]
        gates = (meta[top:2 * top] + meta[2 * top:3 * top]) + meta[3 * top:4 * top]
        tables, slot_weights = pick_table(ids, gates, first.astype(F32), experts, cap, block)
        full = jnp.concatenate(tables, axis=0).astype(BF16)
        tab_ref[p] = full
        got = dot(full, rows_ref[p * 2 * block:(p + 1) * 2 * block, 0:width]).astype(BF16)
        for e in range(experts):
            picked[e, p * n:(p + 1) * n, :] = got[e * n:(e + 1) * n]
            sw_ref[e, p * n:(p + 1) * n, :] = slot_weights[e]
    for e in range(experts):
        gate = dot(picked[e], wg_ref[e])
        up = dot(picked[e], wu_ref[e])
        gate_ref[e] = gate
        up_ref[e] = up
        hidden = (gate * jax.nn.sigmoid(gate) * up).astype(BF16)
        res = dot(hidden, wd_ref[e]) * sw_ref[e]
        res = res.astype(BF16)
        for p in range(pairs):
            weighted[p, e * n:(e + 1) * n, :] = res[p * n:(p + 1) * n]
    for p in range(pairs):
        out_ref[p * 2 * block:(p + 1) * 2 * block, :] = dot(
            tab_ref[p], weighted[p], ((0,), (0,))).astype(BF16)


def bwd_kernel(experts, cap, block, pairs, cot_ref, gate_ref, up_ref, tab_ref, sw_ref,
               wg_ref, wu_ref, wd_ref, out_ref, picked, weighted):
    n = 2 * cap
    tr = ((1,), (1,))
    for p in range(pairs):
        got = dot(tab_ref[p], cot_ref[p * 2 * block:(p + 1) * 2 * block, :])
        for e in range(experts):
            picked[e, p * n:(p + 1) * n, :] = (
                got[e * n:(e + 1) * n] * sw_ref[e, p * n:(p + 1) * n, :]).astype(BF16)
    for e in range(experts):
        hidden_grad = dot(picked[e], wd_ref[e], tr)
        gate = gate_ref[e]
        up = up_ref[e]
        sig = jax.nn.sigmoid(gate)
        pre_grad = (hidden_grad * up * sig * (1.0 + gate * (1.0 - sig))).astype(BF16)
        up_grad = (hidden_grad * gate * sig).astype(BF16)
        res = (dot(pre_grad, wg_ref[e], tr) + dot(up_grad, wu_ref[e], tr)).astype(BF16)
        for p in range(pairs):
            weighted[p, e * n:(e + 1) * n, :] = res[p * n:(p + 1) * n]
    for p in range(pairs):
        out_ref[p * 2 * block:(p + 1) * 2 * block, :] = dot(
            tab_ref[p], weighted[p], ((0,), (0,))).astype(BF16)


def ring_place(chips):
    me = lax.axis_index("expert")
    chip = me // 2
    core = me % 2
    row, col = chip // 2, chip % 2
    place = row + col * (chips - 1 - 2 * row)

    def index(at, which):
        at = (at + 2 * chips) % chips
        back = at // (chips // 2)
        return ((1 - back) * (2 * at) + back * (2 * (chips - 1 - at) + 1)) * 2 + which

    return place, core, index


def enter(peers):
    barrier = pltpu.get_barrier_semaphore()
    for peer in peers:
        pl.semaphore_signal(barrier, inc=1, device_id={"expert": peer},
                            device_id_type=pl.DeviceIdType.MESH)
    pl.semaphore_wait(barrier, len(peers))


def pieces(chips):
    far = chips // 2
    order = []
    for way in range(2):
        row = []
        for d in range(1, far + 1):
            row.append((d, way))
            if d < far:
                row.append((d, 1 - way))
        order.append(row)
    return order


def send_to(src, dst, send_sem, recv_sem, peer):
    return pltpu.make_async_remote_copy(
        src_ref=src, dst_ref=dst, send_sem=send_sem, recv_sem=recv_sem,
        device_id={"expert": peer}, device_id_type=pl.DeviceIdType.MESH)


def gather_kernel(chips, a_ref, b_ref, oa_ref, ob_ref, ring_s, ring_r, pair_s, pair_r, own_s):
    place, core, index = ring_place(chips)
    steps = (1, -1)
    peers = [index(place + 1, core), index(place - 1, core)]
    partner = index(place, 1 - core)
    enter(peers + [partner])
    block = a_ref.shape[0]
    half = block // 2
    ins = (a_ref, b_ref)
    outs = (oa_ref, ob_ref)
    order = pieces(chips)
    count = len(order[0])

    def rows(which, at, h):
        start = pl.multiple_of(index(at, which) * block + h * half, half)
        return pl.ds(start, half)

    waits = []
    own = []
    for j in range(2):
        for x in range(2):
            for way in range(2):
                d, h = order[way][j]
                here = rows(core, place, h)
                copy = send_to(ins[x].at[pl.ds(h * half, half), :], outs[x].at[here, :],
                               ring_s.at[x, way, j], ring_r.at[x, way, j], peers[way])
                copy.start()
                waits.append(copy)
    for x in range(2):
        here = pl.ds(pl.multiple_of(index(place, core) * block, block), block)
        copy = pltpu.make_async_copy(ins[x], outs[x].at[here, :], own_s.at[x])
        copy.start()
        own.append(copy)
        copy = send_to(ins[x], outs[x].at[here, :], pair_s.at[x, 2, 0], pair_r.at[x, 2, 0], partner)
        copy.start()
        waits.append(copy)
    for j in range(count):
        for x in range(2):
            for way in range(2):
                d, h = order[way][j]
                got = outs[x].at[rows(core, place - steps[way] * d, h), :]
                send_to(got, got, ring_s.at[x, way, j], ring_r.at[x, way, j], peers[way]).wait_recv()
                if (d + 1, h) in order[way]:
                    k = order[way].index((d + 1, h))
                    copy = send_to(got, got, ring_s.at[x, way, k], ring_r.at[x, way, k], peers[way])
                    copy.start()
                    waits.append(copy)
                copy = send_to(got, got, pair_s.at[x, way, j], pair_r.at[x, way, j], partner)
                copy.start()
                waits.append(copy)
    for copy in waits:
        copy.wait_send()
    for copy in own:
        copy.wait()
    for x in range(2):
        here = outs[x].at[pl.ds(pl.multiple_of(index(place, 1 - core) * block, block), block), :]
        send_to(here, here, pair_s.at[x, 2, 0], pair_r.at[x, 2, 0], partner).wait_recv()
        for j in range(count):
            for way in range(2):
                d, h = order[way][j]
                here = outs[x].at[rows(1 - core, place - steps[way] * d, h), :]
                send_to(here, here, pair_s.at[x, way, j], pair_r.at[x, way, j], partner).wait_recv()


def ring_gather(a, b, devices):
    chips = devices // 2
    count = chips - 1
    sems = pltpu.SemaphoreType.DMA
    return pl.pallas_call(
        functools.partial(gather_kernel, chips),
        out_shape=[jax.ShapeDtypeStruct((devices * x.shape[0], x.shape[1]), x.dtype) for x in (a, b)],
        in_specs=[pl.BlockSpec(memory_space=pltpu.VMEM)] * 2,
        out_specs=[pl.BlockSpec(memory_space=pl.ANY)] * 2,
        scratch_shapes=[sems((2, 2, count)), sems((2, 2, count)), sems((2, 3, count)),
                        sems((2, 3, count)), sems((2,))],
        compiler_params=pltpu.CompilerParams(collective_id=0, has_side_effects=True),
    )(a, b)


def scatter_kernel(chips, a_ref, b_ref, oa_ref, ob_ref, pair_buf, send_buf, recv_buf,
                   ring_s, ring_r, pair_s, pair_r):
    place, core, index = ring_place(chips)
    steps = (1, -1)
    peers = [index(place + 1, core), index(place - 1, core)]
    partner = index(place, 1 - core)
    enter(peers + [partner])
    block = oa_ref.shape[0]
    half = block // 2
    ins = (a_ref, b_ref)
    outs = (oa_ref, ob_ref)
    far = chips // 2
    order = [row[::-1] for row in pieces(chips)]
    count = len(order[0])
    offsets = [far]
    for d in range(far - 1, 0, -1):
        offsets += [d, -d]
    offsets.append(0)
    slot_of = {o: i for i, o in enumerate(offsets)}
    slot_of[-far] = 0
    pair_copies = {}
    for i, o in enumerate(offsets):
        for x in range(2):
            theirs = pl.ds(pl.multiple_of(index(place + o, 1 - core) * block, block), block)
            copy = send_to(ins[x].at[theirs, :], pair_buf.at[x, i], pair_s.at[x, i],
                           pair_r.at[x, i], partner)
            copy.start()
            pair_copies[x, i] = copy
    arrived = set()

    def need(x, i):
        if (x, i) not in arrived:
            arrived.add((x, i))
            pair_copies[x, i].wait_recv()

    tile = 16

    def add_up(x, o, h, more, write):
        i = slot_of[o]
        need(x, i)
        base = index(place + o, core) * block + h * half

        def body(t, carry):
            r = pl.multiple_of(t * tile, tile)
            total = ins[x][pl.ds(pl.multiple_of(base + r, tile), tile), :].astype(F32)
            total = total + pair_buf[x, i, pl.ds(pl.multiple_of(h * half + r, tile), tile), :].astype(F32)
            for ref in more:
                total = total + recv_buf[ref + (pl.ds(r, tile), slice(None))].astype(F32)
            write(r, total)
            return carry

        lax.fori_loop(0, half // tile, body, 0)

    sends = {}
    for j in range(count):
        for x in range(2):
            for way in range(2):
                d, h = order[way][j]
                more = []
                if (d + 1, h) in order[way]:
                    k = order[way].index((d + 1, h))
                    sends[x, way, k].wait_recv()
                    more.append((x, way, k))

                def write(r, total, x=x, way=way, j=j):
                    send_buf[x, way, j, pl.ds(r, tile), :] = total.astype(BF16)

                add_up(x, steps[way] * d, h, more, write)
                copy = send_to(send_buf.at[x, way, j], recv_buf.at[x, way, j],
                               ring_s.at[x, way, j], ring_r.at[x, way, j], peers[way])
                copy.start()
                sends[x, way, j] = copy
    for x in range(2):
        for h in range(2):
            more = []
            for way in range(2):
                k = order[way].index((1, h))
                sends[x, way, k].wait_recv()
                more.append((x, way, k))

            def write(r, total, x=x, h=h):
                outs[x][pl.ds(pl.multiple_of(h * half + r, tile), tile), :] = total.astype(outs[x].dtype)

            add_up(x, 0, h, more, write)
    for copy in sends.values():
        copy.wait_send()
    for copy in pair_copies.values():
        copy.wait_send()


def ring_scatter(a, b, devices):
    chips = devices // 2
    count = chips - 1
    block, width = a.shape[0] // devices, a.shape[1]
    sems = pltpu.SemaphoreType.DMA
    return pl.pallas_call(
        functools.partial(scatter_kernel, chips),
        out_shape=[jax.ShapeDtypeStruct((block, width), BF16), jax.ShapeDtypeStruct((block, width), F32)],
        in_specs=[pl.BlockSpec(memory_space=pltpu.VMEM)] * 2,
        out_specs=[pl.BlockSpec(memory_space=pltpu.VMEM)] * 2,
        scratch_shapes=[pltpu.VMEM((2, chips, block, width), BF16),
                        pltpu.VMEM((2, 2, count, block // 2, width), BF16),
                        pltpu.VMEM((2, 2, count, block // 2, width), BF16),
                        sems((2, 2, count)), sems((2, 2, count)), sems((2, chips)), sems((2, chips))],
        compiler_params=pltpu.CompilerParams(collective_id=1, has_side_effects=True,
                                             vmem_limit_bytes=62 << 20),
    )(a, b)


def expert_calls(devices, top, weights, block, cap, step_pairs):
    w_gate, w_up, w_down = weights
    experts, width, ff = w_gate.shape
    all_pairs, pair = devices // 2, 2 * block
    grid = (all_pairs // step_pairs,)
    n = 2 * cap
    rows_spec = pl.BlockSpec((step_pairs * pair, width), lambda i: (i, 0))
    whole = lambda a: pl.BlockSpec(a.shape, lambda i: (0, 0, 0), pipeline_mode=pl.Buffered(1))
    pre_spec = pl.BlockSpec((experts, step_pairs * n, ff), lambda i: (0, i, 0))
    tab_spec = pl.BlockSpec((step_pairs, experts * n, pair), lambda i: (i, 0, 0))
    sw_spec = pl.BlockSpec((experts, step_pairs * n, 1), lambda i: (0, i, 0))
    pre_shape = jax.ShapeDtypeStruct((experts, all_pairs * n, ff), F32)
    scratch = [pltpu.VMEM((experts, step_pairs * n, width), BF16),
               pltpu.VMEM((step_pairs, experts * n, width), BF16)]
    params = pltpu.CompilerParams(vmem_limit_bytes=60 << 20)
    flops = 2 * 3 * experts * all_pairs * n * width * ff
    cost = pl.CostEstimate(flops=2 * flops, bytes_accessed=30 << 20, transcendentals=0)

    def fwd(rows):
        return pl.pallas_call(
            functools.partial(fwd_kernel, experts, cap, block, step_pairs, top),
            grid=grid,
            in_specs=[pl.BlockSpec((step_pairs * pair, rows.shape[1]), lambda i: (i, 0)),
                      whole(w_gate), whole(w_up), whole(w_down)],
            out_specs=[rows_spec, pre_spec, pre_spec, tab_spec, sw_spec],
            out_shape=[jax.ShapeDtypeStruct((rows.shape[0], width), BF16), pre_shape, pre_shape,
                       jax.ShapeDtypeStruct((all_pairs, experts * n, pair), BF16),
                       jax.ShapeDtypeStruct((experts, all_pairs * n, 1), F32)],
            scratch_shapes=scratch, compiler_params=params, cost_estimate=cost,
        )(rows, w_gate, w_up, w_down)

    def bwd(cots, gate_pre, up_pre, table, slot_weights):
        return pl.pallas_call(
            functools.partial(bwd_kernel, experts, cap, block, step_pairs),
            grid=grid,
            in_specs=[rows_spec, pre_spec, pre_spec, tab_spec, sw_spec,
                      whole(w_gate), whole(w_up), whole(w_down)],
            out_specs=rows_spec,
            out_shape=jax.ShapeDtypeStruct(cots.shape, BF16),
            scratch_shapes=scratch, compiler_params=params, cost_estimate=cost,
        )(cots, gate_pre, up_pre, table, slot_weights, w_gate, w_up, w_down)

    return fwd, bwd


def local(
    tokens, stream_type, norm_gain, expert_ids, gate_weights, w_gate, w_up, w_down, cotangent
):
    block, width = tokens.shape
    top = expert_ids.shape[1]
    devices = lax.axis_size("expert")
    experts_all = w_gate.shape[0] * devices
    cap = -(-(SLOTS // experts_all) // 8) * 8
    values = tokens.astype(F32)
    inv_rms = lax.rsqrt(jnp.mean(values * values, axis=-1, keepdims=True) + 1e-06)
    unit_rows = values * inv_rms
    gain_rows = jnp.where(stream_type[:, None] == 0, norm_gain[0][None, :], norm_gain[1][None, :])
    normed = (unit_rows * gain_rows).astype(BF16)
    high = lax.reduce_precision(gate_weights, 8, 7)
    middle = lax.reduce_precision(gate_weights - high, 8, 7)
    low = gate_weights - high - middle
    pad = jnp.zeros((block, 128 - 4 * top), BF16)
    normed = jnp.concatenate(
        [normed, expert_ids.astype(BF16), high.astype(BF16), middle.astype(BF16), low.astype(BF16), pad],
        axis=1)
    by_ring = devices % 4 == 0 and devices * block * width * 2 * 2 <= 20 << 20
    if by_ring:
        rows, cots = ring_gather(normed, cotangent, devices)
    else:
        rows = lax.all_gather(normed, "expert", axis=0, tiled=True)
        cots = lax.all_gather(cotangent, "expert", axis=0, tiled=True)
    fwd, bwd = expert_calls(devices, top, (w_gate, w_up, w_down), block, cap, 4)
    out_part, gate_pre, up_pre, table, slot_weights = fwd(rows)
    grad_part = bwd(cots, gate_pre, up_pre, table, slot_weights)
    if by_ring:
        moe_out, normed_grad = ring_scatter(out_part, grad_part, devices)
    else:
        moe_out = lax.psum_scatter(out_part, "expert", scatter_dimension=0, tiled=True)
        normed_grad = lax.psum_scatter(grad_part, "expert", scatter_dimension=0, tiled=True)
    scaled = normed_grad.astype(F32) * gain_rows
    grad_input = inv_rms * (
        scaled - unit_rows * jnp.mean(scaled * unit_rows, axis=-1, keepdims=True)
    )
    return (moe_out, grad_input.astype(BF16))


def solution(mesh):
    in_specs = (
        P(("groups", "expert"), None),
        P(("groups", "expert")),
        P(),
        P(("groups", "expert"), None),
        P(("groups", "expert"), None),
        P("expert", None, None),
        P("expert", None, None),
        P("expert", None, None),
        P(("groups", "expert"), None),
    )
    out_specs = (P(("groups", "expert"), None), P(("groups", "expert"), None))
    return jax.shard_map(local, mesh=mesh, in_specs=in_specs, out_specs=out_specs, check_vma=False)
```

```python
import functools

import jax
import jax.numpy as jnp
from jax import lax
from jax.experimental import pallas as pl
from jax.experimental.pallas import tpu as pltpu
from jax.sharding import PartitionSpec as P

SLOTS = 1280
BF16 = jnp.bfloat16
F32 = jnp.float32


def dot(a, b, dims=((1,), (0,))):
    return lax.dot_general(a, b, (dims, ((), ())), preferred_element_type=F32)


def pick_table(ids, gates, first_expert, experts, cap, block):
    top, pair = ids.shape
    rows_i = lax.broadcasted_iota(jnp.int32, (pair, pair), 0)
    cols_i = lax.broadcasted_iota(jnp.int32, (pair, pair), 1)
    before = ((rows_i < cols_i) & ((rows_i < block) == (cols_i < block))).astype(BF16)
    masks = []
    weights = []
    for e in range(experts):
        hit = ids == (first_expert + e)
        masks.append(jnp.sum(hit.astype(F32), axis=0, keepdims=True))
        weights.append(jnp.sum(jnp.where(hit, gates, 0.0), axis=0, keepdims=True))
    lane = lax.broadcasted_iota(jnp.int32, (1, pair), 1)
    half = jnp.where(lane < block, 0, cap)
    slot_i = lax.broadcasted_iota(jnp.int32, (2 * cap, pair), 0)
    tables = []
    slot_weights = []
    for e in range(experts):
        rank = dot(jnp.broadcast_to(masks[e], (16, pair)).astype(BF16), before)[0:1].astype(jnp.int32)
        slot = jnp.where(masks[e] > 0.5, rank + half, -1)
        table = slot_i == slot
        tables.append(table.astype(F32))
        slot_weights.append(jnp.sum(jnp.where(table, weights[e], 0.0), axis=1, keepdims=True))
    return tables, slot_weights


def fwd_work(experts, cap, block, all_pairs, pairs, top, rows_ref, wg_ref, wu_ref, wd_ref,
             out_ref, gate_ref, up_ref, tab_ref, sw_ref, picked, weighted):
    first = lax.axis_index("expert") * experts
    width = wg_ref.shape[1]
    n = 2 * cap
    pair = 2 * block
    for g in range(0, all_pairs, pairs):
        for p in range(pairs):
            at = slice((g + p) * pair, (g + p + 1) * pair)
            meta = rows_ref[at, width:].astype(F32).T
            ids = meta[0:top]
            gates = (meta[top:2 * top] + meta[2 * top:3 * top]) + meta[3 * top:4 * top]
            tables, slot_weights = pick_table(ids, gates, first.astype(F32), experts, cap, block)
            full = jnp.concatenate(tables, axis=0).astype(BF16)
            tab_ref[g + p] = full
            got = dot(full, rows_ref[at, 0:width]).astype(BF16)
            for e in range(experts):
                picked[e, p * n:(p + 1) * n, :] = got[e * n:(e + 1) * n]
                sw_ref[e, (g + p) * n:(g + p + 1) * n, :] = slot_weights[e]
        yield
        span = slice(g * n, (g + pairs) * n)
        for e in range(experts):
            gate = dot(picked[e], wg_ref[e])
            up = dot(picked[e], wu_ref[e])
            gate_ref[e, span, :] = gate
            up_ref[e, span, :] = up
            hidden = (gate * jax.nn.sigmoid(gate) * up).astype(BF16)
            res = (dot(hidden, wd_ref[e]) * sw_ref[e, span, :]).astype(BF16)
            for p in range(pairs):
                weighted[p, e * n:(e + 1) * n, :] = res[p * n:(p + 1) * n]
            yield
        for p in range(pairs):
            out_ref[(g + p) * pair:(g + p + 1) * pair, :] = dot(
                tab_ref[g + p], weighted[p], ((0,), (0,))).astype(BF16)
        yield


def bwd_work(experts, cap, block, all_pairs, pairs, cot_ref, gate_ref, up_ref, tab_ref, sw_ref,
             wg_ref, wu_ref, wd_ref, out_ref, picked, weighted):
    n = 2 * cap
    pair = 2 * block
    tr = ((1,), (1,))
    for g in range(0, all_pairs, pairs):
        for p in range(pairs):
            got = dot(tab_ref[g + p], cot_ref[(g + p) * pair:(g + p + 1) * pair, :])
            for e in range(experts):
                picked[e, p * n:(p + 1) * n, :] = (
                    got[e * n:(e + 1) * n] * sw_ref[e, (g + p) * n:(g + p + 1) * n, :]).astype(BF16)
        yield
        span = slice(g * n, (g + pairs) * n)
        for e in range(experts):
            hidden_grad = dot(picked[e], wd_ref[e], tr)
            gate = gate_ref[e, span, :]
            up = up_ref[e, span, :]
            sig = jax.nn.sigmoid(gate)
            pre_grad = (hidden_grad * up * sig * (1.0 + gate * (1.0 - sig))).astype(BF16)
            up_grad = (hidden_grad * gate * sig).astype(BF16)
            res = (dot(pre_grad, wg_ref[e], tr) + dot(up_grad, wu_ref[e], tr)).astype(BF16)
            for p in range(pairs):
                weighted[p, e * n:(e + 1) * n, :] = res[p * n:(p + 1) * n]
            yield
        for p in range(pairs):
            out_ref[(g + p) * pair:(g + p + 1) * pair, :] = dot(
                tab_ref[g + p], weighted[p], ((0,), (0,))).astype(BF16)
        yield


def fwd_kernel(experts, cap, block, pairs, top, *refs):
    for unused in fwd_work(experts, cap, block, pairs, pairs, top, *refs):
        pass


def bwd_kernel(experts, cap, block, pairs, *refs):
    for unused in bwd_work(experts, cap, block, pairs, pairs, *refs):
        pass


def ring_place(chips):
    me = lax.axis_index("expert")
    chip = me // 2
    core = me % 2
    row, col = chip // 2, chip % 2
    place = row + col * (chips - 1 - 2 * row)

    def index(at, which):
        at = (at + 2 * chips) % chips
        back = at // (chips // 2)
        return ((1 - back) * (2 * at) + back * (2 * (chips - 1 - at) + 1)) * 2 + which

    return place, core, index


def enter(peers):
    barrier = pltpu.get_barrier_semaphore()
    for peer in peers:
        pl.semaphore_signal(barrier, inc=1, device_id={"expert": peer},
                            device_id_type=pl.DeviceIdType.MESH)
    pl.semaphore_wait(barrier, len(peers))


def pieces(chips):
    far = chips // 2
    order = []
    for way in range(2):
        row = []
        for d in range(1, far + 1):
            row.append((d, way))
            if d < far:
                row.append((d, 1 - way))
        order.append(row)
    return order


def send_to(src, dst, send_sem, recv_sem, peer):
    return pltpu.make_async_remote_copy(
        src_ref=src, dst_ref=dst, send_sem=send_sem, recv_sem=recv_sem,
        device_id={"expert": peer}, device_id_type=pl.DeviceIdType.MESH)


def gather_body(chips, ins, outs, ring_s, ring_r, pair_s, pair_r, own_s, work=()):
    work = iter(work)
    place, core, index = ring_place(chips)
    steps = (1, -1)
    peers = [index(place + 1, core), index(place - 1, core)]
    partner = index(place, 1 - core)
    enter(peers + [partner])
    block = ins[0].shape[0]
    half = block // 2
    order = pieces(chips)
    count = len(order[0])

    def rows(which, at, h):
        start = pl.multiple_of(index(at, which) * block + h * half, half)
        return pl.ds(start, half)

    waits = []
    own = []
    for j in range(2):
        for x in range(len(ins)):
            for way in range(2):
                d, h = order[way][j]
                here = rows(core, place, h)
                copy = send_to(ins[x].at[pl.ds(h * half, half), :], outs[x].at[here, :],
                               ring_s.at[x, way, j], ring_r.at[x, way, j], peers[way])
                copy.start()
                waits.append(copy)
    for x in range(len(ins)):
        here = pl.ds(pl.multiple_of(index(place, core) * block, block), block)
        copy = pltpu.make_async_copy(ins[x], outs[x].at[here, :], own_s.at[x])
        copy.start()
        own.append(copy)
        copy = send_to(ins[x], outs[x].at[here, :], pair_s.at[x, 2, 0], pair_r.at[x, 2, 0], partner)
        copy.start()
        waits.append(copy)
    next(work, None)
    for j in range(count):
        for x in range(len(ins)):
            for way in range(2):
                d, h = order[way][j]
                got = outs[x].at[rows(core, place - steps[way] * d, h), :]
                send_to(got, got, ring_s.at[x, way, j], ring_r.at[x, way, j], peers[way]).wait_recv()
                if (d + 1, h) in order[way]:
                    k = order[way].index((d + 1, h))
                    copy = send_to(got, got, ring_s.at[x, way, k], ring_r.at[x, way, k], peers[way])
                    copy.start()
                    waits.append(copy)
                copy = send_to(got, got, pair_s.at[x, way, j], pair_r.at[x, way, j], partner)
                copy.start()
                waits.append(copy)
        next(work, None)
    for unused in work:
        pass
    for copy in waits:
        copy.wait_send()
    for copy in own:
        copy.wait()
    for x in range(len(ins)):
        here = outs[x].at[pl.ds(pl.multiple_of(index(place, 1 - core) * block, block), block), :]
        send_to(here, here, pair_s.at[x, 2, 0], pair_r.at[x, 2, 0], partner).wait_recv()
        for j in range(count):
            for way in range(2):
                d, h = order[way][j]
                here = outs[x].at[rows(1 - core, place - steps[way] * d, h), :]
                send_to(here, here, pair_s.at[x, way, j], pair_r.at[x, way, j], partner).wait_recv()


def gather_sems(arrays, count):
    sems = pltpu.SemaphoreType.DMA
    return [sems((arrays, 2, count)), sems((arrays, 2, count)), sems((arrays, 3, count)),
            sems((arrays, 3, count)), sems((arrays,))]


def gather_kernel(chips, a_ref, oa_ref, *scratch):
    gather_body(chips, (a_ref,), (oa_ref,), *scratch)


VM = pl.BlockSpec(memory_space=pltpu.VMEM)
ANY = pl.BlockSpec(memory_space=pl.ANY)


def ring_gather(a, devices):
    chips = devices // 2
    return pl.pallas_call(
        functools.partial(gather_kernel, chips),
        out_shape=jax.ShapeDtypeStruct((devices * a.shape[0], a.shape[1]), a.dtype),
        in_specs=[VM], out_specs=ANY,
        scratch_shapes=gather_sems(1, chips - 1),
        compiler_params=pltpu.CompilerParams(collective_id=0, has_side_effects=True),
    )(a)


def fwd_gather_kernel(chips, experts, cap, block, pairs, top, cot_ref, rows_ref, wg_ref, wu_ref, wd_ref,
                      cots_ref, out_ref, gate_ref, up_ref, tab_ref, sw_ref, rows, wg, wu, wd,
                      picked, weighted, load_s, *sems):
    loads = [pltpu.make_async_copy(src, dst, load_s.at[i]) for i, (src, dst) in enumerate(
        ((rows_ref, rows), (wg_ref, wg), (wu_ref, wu), (wd_ref, wd)))]
    for load in loads:
        load.start()

    def work():
        for load in loads:
            load.wait()
        yield from fwd_work(experts, cap, block, chips, pairs, top, rows, wg, wu, wd,
                            out_ref, gate_ref, up_ref, tab_ref, sw_ref, picked, weighted)

    gather_body(chips, (cot_ref,), (cots_ref,), *sems, work=work())


def fwd_gather(cot, rows, weights, cap, top, devices, pairs):
    chips = devices // 2
    experts, width, ff = weights[0].shape
    block = cot.shape[0]
    n = 2 * cap
    pre = jax.ShapeDtypeStruct((experts, chips * n, ff), F32)
    return pl.pallas_call(
        functools.partial(fwd_gather_kernel, chips, experts, cap, block, pairs, top),
        out_shape=[jax.ShapeDtypeStruct((devices * block, width), BF16),
                   jax.ShapeDtypeStruct((devices * block, width), BF16), pre, pre,
                   jax.ShapeDtypeStruct((chips, experts * n, 2 * block), BF16),
                   jax.ShapeDtypeStruct((experts, chips * n, 1), F32)],
        in_specs=[VM, ANY, ANY, ANY, ANY],
        out_specs=[ANY, VM, VM, VM, VM, VM],
        scratch_shapes=[pltpu.VMEM(rows.shape, BF16)] + [pltpu.VMEM(w.shape, BF16) for w in weights] + [
            pltpu.VMEM((experts, pairs * n, width), BF16), pltpu.VMEM((pairs, experts * n, width), BF16),
            pltpu.SemaphoreType.DMA((4,))] + gather_sems(1, chips - 1),
        compiler_params=pltpu.CompilerParams(collective_id=2, has_side_effects=True,
                                             vmem_limit_bytes=60 << 20),
    )(cot, rows, *weights)


def scatter_body(chips, ins, outs, pair_buf, send_buf, recv_buf, ring_s, ring_r, pair_s, pair_r,
                 work=()):
    work = iter(work)
    place, core, index = ring_place(chips)
    steps = (1, -1)
    peers = [index(place + 1, core), index(place - 1, core)]
    partner = index(place, 1 - core)
    enter(peers + [partner])
    block = outs[0].shape[0]
    half = block // 2
    far = chips // 2
    order = [row[::-1] for row in pieces(chips)]
    count = len(order[0])
    offsets = [far]
    for d in range(far - 1, 0, -1):
        offsets += [d, -d]
    offsets.append(0)
    slot_of = {o: i for i, o in enumerate(offsets)}
    slot_of[-far] = 0
    pair_copies = {}
    for i, o in enumerate(offsets):
        for x in range(len(ins)):
            theirs = pl.ds(pl.multiple_of(index(place + o, 1 - core) * block, block), block)
            copy = send_to(ins[x].at[theirs, :], pair_buf.at[x, i], pair_s.at[x, i],
                           pair_r.at[x, i], partner)
            copy.start()
            pair_copies[x, i] = copy
    arrived = set()

    def need(x, i):
        if (x, i) not in arrived:
            arrived.add((x, i))
            pair_copies[x, i].wait_recv()

    tile = 16

    def add_up(x, o, h, more, write):
        i = slot_of[o]
        need(x, i)
        base = index(place + o, core) * block + h * half

        def body(t, carry):
            r = pl.multiple_of(t * tile, tile)
            total = ins[x][pl.ds(pl.multiple_of(base + r, tile), tile), :].astype(F32)
            total = total + pair_buf[x, i, pl.ds(pl.multiple_of(h * half + r, tile), tile), :].astype(F32)
            for ref in more:
                total = total + recv_buf[ref + (pl.ds(r, tile), slice(None))].astype(F32)
            write(r, total)
            return carry

        lax.fori_loop(0, half // tile, body, 0)

    sends = {}
    for j in range(count):
        for x in range(len(ins)):
            for way in range(2):
                d, h = order[way][j]
                more = []
                if (d + 1, h) in order[way]:
                    k = order[way].index((d + 1, h))
                    sends[x, way, k].wait_recv()
                    more.append((x, way, k))

                def write(r, total, x=x, way=way, j=j):
                    send_buf[x, way, j, pl.ds(r, tile), :] = total.astype(BF16)

                add_up(x, steps[way] * d, h, more, write)
                copy = send_to(send_buf.at[x, way, j], recv_buf.at[x, way, j],
                               ring_s.at[x, way, j], ring_r.at[x, way, j], peers[way])
                copy.start()
                sends[x, way, j] = copy
        next(work, None)
    for unused in work:
        pass
    for x in range(len(ins)):
        for h in range(2):
            more = []
            for way in range(2):
                k = order[way].index((1, h))
                sends[x, way, k].wait_recv()
                more.append((x, way, k))

            def write(r, total, x=x, h=h):
                outs[x][pl.ds(pl.multiple_of(h * half + r, tile), tile), :] = total.astype(outs[x].dtype)

            add_up(x, 0, h, more, write)
    for copy in sends.values():
        copy.wait_send()
    for copy in pair_copies.values():
        copy.wait_send()


def scatter_scratch(arrays, chips, block, width):
    count = chips - 1
    sems = pltpu.SemaphoreType.DMA
    return [pltpu.VMEM((arrays, chips, block, width), BF16),
            pltpu.VMEM((arrays, 2, count, block // 2, width), BF16),
            pltpu.VMEM((arrays, 2, count, block // 2, width), BF16),
            sems((arrays, 2, count)), sems((arrays, 2, count)), sems((arrays, chips)),
            sems((arrays, chips))]


def scatter_kernel(chips, a_ref, oa_ref, *scratch):
    scatter_body(chips, (a_ref,), (oa_ref,), *scratch)


def ring_scatter(a, devices):
    chips = devices // 2
    block, width = a.shape[0] // devices, a.shape[1]
    return pl.pallas_call(
        functools.partial(scatter_kernel, chips),
        out_shape=jax.ShapeDtypeStruct((block, width), F32),
        in_specs=[VM], out_specs=VM,
        scratch_shapes=scatter_scratch(1, chips, block, width),
        compiler_params=pltpu.CompilerParams(collective_id=1, has_side_effects=True,
                                             vmem_limit_bytes=40 << 20),
    )(a)


def bwd_scatter_kernel(chips, experts, cap, block, pairs, part_ref, cots_ref, gate_ref, up_ref, tab_ref,
                       sw_ref, wg_ref, wu_ref, wd_ref, moe_ref, out_ref, cots, wg, wu, wd,
                       picked, weighted, load_s, *scratch):
    loads = [pltpu.make_async_copy(src, dst, load_s.at[i]) for i, (src, dst) in enumerate(
        ((cots_ref, cots), (wg_ref, wg), (wu_ref, wu), (wd_ref, wd)))]
    for load in loads:
        load.start()

    def work():
        for load in loads:
            load.wait()
        yield from bwd_work(experts, cap, block, chips, pairs, cots, gate_ref, up_ref, tab_ref, sw_ref,
                            wg, wu, wd, out_ref, picked, weighted)

    scatter_body(chips, (part_ref,), (moe_ref,), *scratch, work=work())


def bwd_scatter(part, cots, gate_pre, up_pre, table, slot_weights, weights, cap, devices, pairs):
    chips = devices // 2
    experts, width, ff = weights[0].shape
    block = part.shape[0] // devices
    n = 2 * cap
    return pl.pallas_call(
        functools.partial(bwd_scatter_kernel, chips, experts, cap, block, pairs),
        out_shape=[jax.ShapeDtypeStruct((block, width), BF16), jax.ShapeDtypeStruct(part.shape, BF16)],
        in_specs=[VM, ANY, VM, VM, VM, VM, ANY, ANY, ANY],
        out_specs=[VM, VM],
        scratch_shapes=[pltpu.VMEM(cots.shape, BF16)] + [pltpu.VMEM(w.shape, BF16) for w in weights] + [
            pltpu.VMEM((experts, pairs * n, width), BF16), pltpu.VMEM((pairs, experts * n, width), BF16),
            pltpu.SemaphoreType.DMA((4,))] + scatter_scratch(1, chips, block, width),
        compiler_params=pltpu.CompilerParams(collective_id=3, has_side_effects=True,
                                             vmem_limit_bytes=67043328),
    )(part, cots, gate_pre, up_pre, table, slot_weights, *weights)


def expert_calls(devices, top, weights, block, cap, step_pairs):
    w_gate, w_up, w_down = weights
    experts, width, ff = w_gate.shape
    all_pairs, pair = devices // 2, 2 * block
    grid = (all_pairs // step_pairs,)
    n = 2 * cap
    rows_spec = pl.BlockSpec((step_pairs * pair, width), lambda i: (i, 0))
    whole = lambda a: pl.BlockSpec(a.shape, lambda i: (0, 0, 0), pipeline_mode=pl.Buffered(1))
    pre_spec = pl.BlockSpec((experts, step_pairs * n, ff), lambda i: (0, i, 0))
    tab_spec = pl.BlockSpec((step_pairs, experts * n, pair), lambda i: (i, 0, 0))
    sw_spec = pl.BlockSpec((experts, step_pairs * n, 1), lambda i: (0, i, 0))
    pre_shape = jax.ShapeDtypeStruct((experts, all_pairs * n, ff), F32)
    scratch = [pltpu.VMEM((experts, step_pairs * n, width), BF16),
               pltpu.VMEM((step_pairs, experts * n, width), BF16)]
    params = pltpu.CompilerParams(vmem_limit_bytes=60 << 20)
    flops = 2 * 3 * experts * all_pairs * n * width * ff
    cost = pl.CostEstimate(flops=2 * flops, bytes_accessed=30 << 20, transcendentals=0)

    def fwd(rows):
        return pl.pallas_call(
            functools.partial(fwd_kernel, experts, cap, block, step_pairs, top),
            grid=grid,
            in_specs=[pl.BlockSpec((step_pairs * pair, rows.shape[1]), lambda i: (i, 0)),
                      whole(w_gate), whole(w_up), whole(w_down)],
            out_specs=[rows_spec, pre_spec, pre_spec, tab_spec, sw_spec],
            out_shape=[jax.ShapeDtypeStruct((rows.shape[0], width), BF16), pre_shape, pre_shape,
                       jax.ShapeDtypeStruct((all_pairs, experts * n, pair), BF16),
                       jax.ShapeDtypeStruct((experts, all_pairs * n, 1), F32)],
            scratch_shapes=scratch, compiler_params=params, cost_estimate=cost,
        )(rows, w_gate, w_up, w_down)

    def bwd(cots, gate_pre, up_pre, table, slot_weights):
        return pl.pallas_call(
            functools.partial(bwd_kernel, experts, cap, block, step_pairs),
            grid=grid,
            in_specs=[rows_spec, pre_spec, pre_spec, tab_spec, sw_spec,
                      whole(w_gate), whole(w_up), whole(w_down)],
            out_specs=rows_spec,
            out_shape=jax.ShapeDtypeStruct(cots.shape, BF16),
            scratch_shapes=scratch, compiler_params=params, cost_estimate=cost,
        )(cots, gate_pre, up_pre, table, slot_weights, w_gate, w_up, w_down)

    return fwd, bwd


def local(
    tokens, stream_type, norm_gain, expert_ids, gate_weights, w_gate, w_up, w_down, cotangent
):
    block, width = tokens.shape
    top = expert_ids.shape[1]
    devices = lax.axis_size("expert")
    experts_all = w_gate.shape[0] * devices
    cap = -(-(SLOTS // experts_all) // 8) * 8
    values = tokens.astype(F32)
    inv_rms = lax.rsqrt(jnp.mean(values * values, axis=-1, keepdims=True) + 1e-06)
    unit_rows = values * inv_rms
    gain_rows = jnp.where(stream_type[:, None] == 0, norm_gain[0][None, :], norm_gain[1][None, :])
    normed = (unit_rows * gain_rows).astype(BF16)
    high = lax.reduce_precision(gate_weights, 8, 7)
    middle = lax.reduce_precision(gate_weights - high, 8, 7)
    low = gate_weights - high - middle
    pad = jnp.zeros((block, 128 - 4 * top), BF16)
    normed = jnp.concatenate(
        [normed, expert_ids.astype(BF16), high.astype(BF16), middle.astype(BF16), low.astype(BF16), pad],
        axis=1)
    by_ring = devices % 4 == 0 and devices * block * width * 2 * 2 <= 20 << 20
    weights = (w_gate, w_up, w_down)
    if by_ring:
        rows = ring_gather(normed, devices)
        cots, out_part, *saved = fwd_gather(cotangent, rows, weights, cap, top, devices, 4)
        moe_out, grad_part = bwd_scatter(out_part, cots, *saved, weights, cap, devices, 2)
        normed_grad = ring_scatter(grad_part, devices)
    else:
        rows = lax.all_gather(normed, "expert", axis=0, tiled=True)
        cots = lax.all_gather(cotangent, "expert", axis=0, tiled=True)
        fwd, bwd = expert_calls(devices, top, weights, block, cap, 4)
        out_part, *saved = fwd(rows)
        moe_out = lax.psum_scatter(out_part, "expert", scatter_dimension=0, tiled=True)
        grad_part = bwd(cots, *saved)
        normed_grad = lax.psum_scatter(grad_part, "expert", scatter_dimension=0, tiled=True)
    scaled = normed_grad.astype(F32) * gain_rows
    grad_input = inv_rms * (
        scaled - unit_rows * jnp.mean(scaled * unit_rows, axis=-1, keepdims=True)
    )
    return (moe_out, grad_input.astype(BF16))


def solution(mesh):
    in_specs = (
        P(("groups", "expert"), None),
        P(("groups", "expert")),
        P(),
        P(("groups", "expert"), None),
        P(("groups", "expert"), None),
        P("expert", None, None),
        P("expert", None, None),
        P("expert", None, None),
        P(("groups", "expert"), None),
    )
    out_specs = (P(("groups", "expert"), None), P(("groups", "expert"), None))
    return jax.shard_map(local, mesh=mesh, in_specs=in_specs, out_specs=out_specs, check_vma=False)
```
